32 devices in a mesh: panel: 16 (over z, x, core), freq: 2 (over y).
Axes of the slice: x: 2, y: 2, z: 4, core: 2. Of those that a mesh axis runs over, the one named last changes fastest.
Arguments:
- sources: bfloat16 [2, 4096, 1024], P(None, ('panel', 'freq')), may hold values from -6 to 6
- panel_pos: float32 [3, 4096], P(None, 'panel'), may hold values from -30 to 30
- normal_angles: float32 [2, 4096], P(None, 'panel'), may hold values from -3.140625 to 3.140625
- observer_angles: float32 [2, 2048], replicated, may hold values from -3.140625 to 3.140625
- absorption: float32 [64, 16], replicated, may hold values from 0.05 to 1
- ray_count: int32 [131072], P('panel'), may hold values from 1 to 8
- ray_layer: int32 [8, 131072], P(None, 'panel'), may hold values from 0 to 15
- ray_length: float32 [8, 131072], P(None, 'panel'), may hold values from 0.1 to 1
- ray_weight: float32 [131072], P('panel'), may hold values from 0.01 to 0.1
- ray_ground: int32 [131072], P('panel'), may hold values from 0 to 4095
Outputs:
- obs_spectrum: float32 [2048, 128], P('panel', 'freq')
- ground_power: float32 [64, 4096], P(None, 'panel')
The draws below stay inside these ranges and needn't reach their ends.
All inputs are finite; a program needn't handle non-finite values.
Results may differ from the reference program's by a relative error of at most 0.0026.
Values may be sent and summed in bfloat16 or wider, within the bound.
A program may use at most 64 MiB of HBM per device.

```python
import math
import jax
import jax.numpy as jnp
from jax import lax

SAMPLES = 1024
FREQS = 64
BIN0 = 32
OBS = 2048
PANELS = 4096
RAYS = 64
RAY_ROWS = 131072
SEGS = 8
LAYERS = 16
GROUND = 4096


def plant(array, rng, least, top_value):
    longest = array.shape.index(max(array.shape))
    spots = []
    for shift in (0, 1):
        where = [jax.random.randint(jax.random.fold_in(rng, axis), (), 0, length) for axis, length in enumerate(array.shape)]
        where[longest] = (where[longest] + shift) % array.shape[longest]
        spots.append(tuple(where))
    return array.at[spots[0]].set(least).at[spots[1]].set(top_value)


def level_of(own_key, extent, split, low, high):
    loudness = 1.0
    for position, parts in split:
        draws = jax.random.uniform(jax.random.fold_in(jax.random.fold_in(own_key, 6), position), (parts,), jnp.float32, low / len(split), high / len(split))
        loudness = loudness * jnp.repeat(jnp.exp(draws), extent[position] // parts).reshape((-1,) + (1,) * (len(extent) - 1 - position))
    return loudness


def gaussian(rng, dims, width, reach, split=(), held_as=jnp.bfloat16):
    factor_of = level_of(rng, dims, split, -0.22, 0.18) if split else 1.0
    values = jax.random.normal(rng, dims, jnp.float32) * width * factor_of
    return jnp.minimum(jnp.maximum(values, -reach), reach).astype(held_as)


def setup_inputs(seed: int = 0) -> dict:
    splits = jax.random.split(jax.random.key(seed), 11)
    sources = gaussian(splits[0], (2, PANELS, SAMPLES), 1.0, 6.0, ((1, 32),))
    panel_pos = jnp.clip(jax.random.uniform(splits[1], (3, PANELS), jnp.float32, -30.0, 30.0) * level_of(splits[1], (3, PANELS), ((1, 16),), -0.4, 0.0), -30.0, 30.0)
    normal_angles = jnp.clip(jax.random.uniform(splits[2], (2, PANELS), jnp.float32, -3.140625, 3.140625), -3.140625, 3.140625)
    observer_angles = jnp.clip(jax.random.uniform(splits[3], (2, OBS), jnp.float32, -3.140625, 3.140625), -3.140625, 3.140625)
    absorption = jnp.clip(jnp.exp(jax.random.uniform(splits[4], (FREQS, LAYERS), jnp.float32, math.log(0.05), math.log(1.0))), 0.05, 1.0)
    ray_count = plant(jax.random.randint(splits[5], (RAY_ROWS,), 1, SEGS + 1), jax.random.fold_in(splits[5], 1), 1, SEGS).astype(jnp.int32)
    ray_layer = plant(jax.random.randint(splits[6], (SEGS, RAY_ROWS), 0, LAYERS), jax.random.fold_in(splits[6], 1), 0, LAYERS - 1).astype(jnp.int32)
    ray_length = jnp.clip(jnp.exp(math.log(1.0) - 2.3025851 * jax.random.uniform(splits[7], (SEGS, RAY_ROWS), jnp.float32) ** level_of(splits[7], (SEGS, RAY_ROWS), ((1, 16),), -0.2, 0.2)), 0.1, 1.0)
    ray_weight = jnp.clip(jnp.exp(math.log(0.1) - 2.3025851 * jax.random.uniform(splits[8], (RAY_ROWS,), jnp.float32) ** level_of(splits[8], (RAY_ROWS,), ((0, 16),), -0.2, 0.2)), 0.01, 0.1)
    ray_ground = plant(jax.random.randint(splits[9], (RAY_ROWS,), 0, GROUND), jax.random.fold_in(splits[9], 1), 0, GROUND - 1).astype(jnp.int32)
    return dict(sources=sources, panel_pos=panel_pos, normal_angles=normal_angles, observer_angles=observer_angles, absorption=absorption, ray_count=ray_count, ray_layer=ray_layer, ray_length=ray_length, ray_weight=ray_weight, ray_ground=ray_ground)


RADIUS = 150.0
GAIN = 3.0

def dft_table(samples, first_bin, nfreqs):
    sample_index = jnp.arange(samples, dtype=jnp.int32)
    bin_index = first_bin + jnp.arange(nfreqs, dtype=jnp.int32)
    phase_turns = sample_index[:, None] * bin_index[None, :] % samples
    phase_angle = 2.0 * math.pi / samples * phase_turns.astype(jnp.float32)
    window = 0.5 - 0.5 * jnp.cos(2.0 * math.pi / samples * sample_index.astype(jnp.float32))
    weighting = (window / math.sqrt(samples))[:, None]
    stacked = jnp.stack([weighting * jnp.cos(phase_angle), -weighting * jnp.sin(phase_angle)], axis=2)
    return stacked.reshape(samples, 2 * nfreqs).astype(jnp.bfloat16)

def sphere_points(angles, radius, downward):
    polar_angle = angles[0]
    azimuth = angles[1]
    height = -jnp.cos(polar_angle) if downward else jnp.cos(polar_angle)
    return radius * jnp.stack([jnp.sin(polar_angle) * jnp.cos(azimuth), jnp.sin(polar_angle) * jnp.sin(azimuth), height])

def radiate(points, panel_pos, normals, wavenumbers, spectra, weighting):
    offset = points[:, :, None] - panel_pos[:, None, :]
    distance = jnp.sqrt(lax.optimization_barrier(jnp.sum(offset * offset, axis=0)))
    inverse = 1.0 / distance
    cosine = lax.optimization_barrier(jnp.sum(offset * normals[:, None, :], axis=0)) * inverse
    amplitude = RADIUS * weighting * inverse
    freq_count = wavenumbers.shape[0]
    per_freq = spectra.reshape(2, spectra.shape[1], freq_count, 2).transpose(2, 0, 1, 3)

    def one_freq(inputs):
        wavenumber, coeffs = inputs
        phase = wavenumber * distance
        cos_part = amplitude * jnp.cos(phase)
        sin_part = -amplitude * jnp.sin(phase)
        dip_real = cosine * (cos_part * inverse - wavenumber * sin_part)
        dip_imag = cosine * (sin_part * inverse + wavenumber * cos_part)
        mono_real = (-wavenumber * coeffs[0, :, 1])[None, :]
        mono_imag = (wavenumber * coeffs[0, :, 0])[None, :]
        load_real = coeffs[1, :, 0][None, :]
        load_imag = coeffs[1, :, 1][None, :]
        real_sum = lax.optimization_barrier(jnp.sum(cos_part * mono_real - sin_part * mono_imag + dip_real * load_real - dip_imag * load_imag, axis=1))
        imag_sum = lax.optimization_barrier(jnp.sum(cos_part * mono_imag + sin_part * mono_real + dip_real * load_imag + dip_imag * load_real, axis=1))
        return jnp.stack([real_sum, imag_sum], axis=1)
    result = lax.map(one_freq, (wavenumbers, per_freq))
    return result.transpose(1, 0, 2).reshape(points.shape[1], 2 * freq_count)

def layer_lengths(ray_count, ray_layer, ray_length):
    seg_rows = ray_layer.shape[0]
    segment = jnp.arange(seg_rows, dtype=jnp.int32)[:, None]
    used = jnp.where(segment < ray_count.reshape(1, -1), ray_length.reshape(seg_rows, -1), 0.0)
    layer_ids = jnp.arange(LAYERS, dtype=jnp.int32)[None, :, None]
    matches = ray_layer.reshape(seg_rows, 1, -1) == layer_ids
    return lax.optimization_barrier(jnp.sum(jnp.where(matches, used[:, None, :], 0.0), axis=0))

def ground_energy(power_rows, absorption, lengths, ray_weight, ray_ground, ground_count):
    optical_depth = jnp.dot(absorption, lengths, precision=lax.Precision.HIGHEST)
    freq_count = power_rows.shape[0]
    obs_count = power_rows.shape[1]
    shaped = optical_depth.reshape(freq_count, obs_count, RAYS)
    energy = power_rows[:, :, None] * ray_weight.reshape(1, obs_count, RAYS) * jnp.exp(-shaped)
    empty = jnp.zeros((freq_count, ground_count), jnp.float32)
    return empty.at[:, ray_ground.reshape(-1)].add(energy.reshape(freq_count, -1))

def reference(sources, panel_pos, normal_angles, observer_angles, absorption, ray_count, ray_layer, ray_length, ray_weight, ray_ground):
    transform_table = dft_table(SAMPLES, BIN0, FREQS)
    spectra = jnp.dot(sources.reshape(-1, SAMPLES), transform_table, preferred_element_type=jnp.float32)
    spectra = spectra.reshape(2, -1, 2 * FREQS)
    wavenumbers = (BIN0 + jnp.arange(FREQS, dtype=jnp.int32)).astype(jnp.float32) * (2.0 * math.pi / SAMPLES)
    points = sphere_points(observer_angles, RADIUS, True)
    normals = sphere_points(normal_angles, 1.0, False)
    weighting = GAIN / math.sqrt(PANELS)
    obs_spectrum = radiate(points, panel_pos, normals, wavenumbers, spectra, weighting)
    power_rows = (obs_spectrum[:, 0::2] * obs_spectrum[:, 0::2] + obs_spectrum[:, 1::2] * obs_spectrum[:, 1::2]).T
    lengths = layer_lengths(ray_count, ray_layer, ray_length)
    ground_power = ground_energy(power_rows, absorption, lengths, ray_weight, ray_ground, GROUND)
    return (obs_spectrum, ground_power)
```

```python
import functools
import math

import jax
import jax.numpy as jnp
import numpy as np
from jax import lax
from jax.experimental import pallas as pl
from jax.experimental.pallas import tpu as pltpu
from jax.sharding import PartitionSpec as P

SAMPLES = 1024
BIN0 = 32
RADIUS = 150.0
GAIN = 3.0
GROUND = 4096
TILE = 16
MESH = pl.DeviceIdType.MESH
VMEM = pltpu.MemorySpace.VMEM


def dft_rows(samples, first_bin, groups, per_group):
    index = np.arange(samples)
    bins = first_bin + np.arange(groups * per_group)
    angle = 2.0 * np.pi / samples * (bins[:, None] * index[None, :] % samples)
    window = (0.5 - 0.5 * np.cos(2.0 * np.pi / samples * index)) / math.sqrt(samples)
    rows = np.stack([window * np.cos(angle), -window * np.sin(angle)])
    rows = rows.reshape(2, groups, per_group, samples).transpose(1, 0, 2, 3)
    return rows.reshape(-1, samples).astype(np.float32)


def sphere_points(angles, downward):
    polar, azimuth = angles[0], angles[1]
    height = -jnp.cos(polar) if downward else jnp.cos(polar)
    return jnp.stack(
        [jnp.sin(polar) * jnp.cos(azimuth), jnp.sin(polar) * jnp.sin(azimuth), height]
    )


def sincos_turns(turns):
    part = turns - jnp.round(turns)
    square = part * part
    sine = jnp.float32(-(math.pi**11) / math.factorial(11))
    for power in (9, 7, 5, 3, 1):
        sign = 1.0 if power % 4 == 1 else -1.0
        sine = sine * square + sign * math.pi**power / math.factorial(power)
    sine = sine * part
    cosine = jnp.float32(math.pi**12 / math.factorial(12))
    for power in (10, 8, 6, 4, 2, 0):
        sign = 1.0 if power % 4 == 0 else -1.0
        cosine = cosine * square + sign * math.pi**power / math.factorial(power)
    return 1.0 - 2.0 * sine * sine, 2.0 * sine * cosine


def radiate_kernel(freqs, panels, width, blocks, first_ref, pos_ref, points_ref, coef_ref,
                   out_ref, planes_a, planes_b, stage):
    tiles = panels // TILE
    half = width // out_ref.shape[2]
    lanes = out_ref.shape[2]

    def generate(planes, block, tile):
        rows = pl.ds(pl.multiple_of(tile * TILE, TILE), TILE)
        cols = pl.ds(pl.multiple_of(block * width, width), width)
        total = None
        for axis in range(3):
            diff = points_ref[axis : axis + 1, cols] - pos_ref[rows, axis : axis + 1]
            total = diff * diff if total is None else total + diff * diff
        inverse = lax.rsqrt(total)
        inverse = inverse * (1.5 - 0.5 * total * inverse * inverse)
        turn = total * inverse * jnp.float32(RADIUS / SAMPLES)
        cos_step, sin_step = sincos_turns(turn)
        cos_now, sin_now = sincos_turns(turn * first_ref[0:1, 0:1])
        square = inverse * inverse
        cube = square * inverse
        cos_next = cos_now * cos_step - sin_now * sin_step
        sin_next = sin_now * cos_step + cos_now * sin_step
        twice = 2.0 * cos_step
        before = [cos_now * cube, sin_now * cube, cos_now * square, sin_now * square]
        current = [cos_next * cube, sin_next * cube, cos_next * square, sin_next * square]
        for f in range(freqs):
            for part in range(4):
                at = pl.ds(pl.multiple_of(part * panels + tile * TILE, TILE), TILE)
                planes[f, at, :] = before[part].astype(jnp.bfloat16)
            if f + 1 < freqs:
                before, current = current, [
                    twice * now - old for now, old in zip(current, before)
                ]

    def contract(planes, block, f):
        cols = pl.ds(pl.multiple_of(block * width, width), width)
        product = jnp.dot(coef_ref[f], planes[f], preferred_element_type=jnp.float32)
        product = (product[0:8] + product[8:16]) * points_ref[8:16, cols]
        product = product + pltpu.roll(product, 1, axis=0)
        product = product + pltpu.roll(product, 2, axis=0)
        for side in range(half):
            stage[side, pl.ds(pl.multiple_of(f * 8, 8), 8), :] = product[
                :, side * lanes : (side + 1) * lanes
            ]

    def finish(block):
        for part in range(2):
            for side in range(half):
                out_ref[block * half + side, part * freqs : (part + 1) * freqs, :] = stage[
                    side, pl.ds(4 * part + 3, freqs, 8), :
                ]

    def phase(generated, generated_block, used, used_block):
        if generated is not None and used is not None and freqs % tiles == 0:
            each = freqs // tiles

            def both(tile, carry):
                for n in range(each):
                    contract(used, used_block, tile * each + n)
                generate(generated, generated_block, tile)
                return carry

            lax.fori_loop(0, tiles, both, 0)
            finish(used_block)
            return
        if generated is not None:

            def only_generate(tile, carry):
                generate(generated, generated_block, tile)
                return carry

            lax.fori_loop(0, tiles, only_generate, 0)
        if used is not None:

            def only_contract(f, carry):
                contract(used, used_block, f)
                return carry

            lax.fori_loop(0, freqs, only_contract, 0)
            finish(used_block)

    phase(planes_a, 0, None, None)

    def pair(step, carry):
        phase(planes_b, 2 * step + 1, planes_a, 2 * step)
        phase(planes_a, 2 * step + 2, planes_b, 2 * step + 1)
        return carry

    lax.fori_loop(0, blocks // 2 - 1, pair, 0)
    phase(planes_b, blocks - 1, planes_a, blocks - 2)
    phase(None, None, planes_b, blocks - 1)


def radiate(first, positions, points, coefs, owners):
    freqs, _, depth = coefs.shape
    panels = depth // 4
    observers = points.shape[1]
    lanes = observers // owners
    width = 256
    blocks = observers // width
    return pl.pallas_call(
        functools.partial(radiate_kernel, freqs, panels, width, blocks),
        out_shape=jax.ShapeDtypeStruct((owners, 2 * freqs, lanes), jnp.float32),
        in_specs=[pl.BlockSpec(memory_space=VMEM)] * 4,
        out_specs=pl.BlockSpec(memory_space=VMEM),
        scratch_shapes=[
            pltpu.VMEM((freqs, depth, width), jnp.bfloat16),
            pltpu.VMEM((freqs, depth, width), jnp.bfloat16),
            pltpu.VMEM((width // lanes, freqs * 8, lanes), jnp.float32),
        ],
        compiler_params=pltpu.CompilerParams(vmem_limit_bytes=60 * 1024 * 1024),
        name="radiate",
    )(first, positions, points, coefs)


def enter(axis, count):
    barrier = pltpu.get_barrier_semaphore()
    me = lax.axis_index(axis)
    for step in range(1, count):
        pl.semaphore_signal(
            barrier, inc=1, device_id={axis: lax.rem(me + step, count)}, device_id_type=MESH
        )
    return barrier


def scatter_sum_kernel(owners, part_ref, out_ref, landed, send_sem, recv_sem):
    me = lax.axis_index("panel")
    pl.semaphore_wait(enter("panel", owners), owners - 1)
    copies = []
    for step in range(1, owners):
        peer = lax.rem(me + step, owners)
        copies.append(
            pltpu.make_async_remote_copy(
                src_ref=part_ref.at[peer],
                dst_ref=landed.at[step],
                send_sem=send_sem.at[step],
                recv_sem=recv_sem.at[step],
                device_id={"panel": peer},
                device_id_type=MESH,
            )
        )
        copies[-1].start()
    total = part_ref[me]
    for step in range(1, owners):
        copies[step - 1].wait_recv()
        total = total + landed[step]
    out_ref[...] = total
    for copy in copies:
        copy.wait_send()


def scatter_sum(parts):
    owners, rows, lanes = parts.shape
    return pl.pallas_call(
        functools.partial(scatter_sum_kernel, owners),
        out_shape=jax.ShapeDtypeStruct((rows, lanes), jnp.float32),
        in_specs=[pl.BlockSpec(memory_space=VMEM)],
        out_specs=pl.BlockSpec(memory_space=VMEM),
        scratch_shapes=[
            pltpu.VMEM((owners, rows, lanes), jnp.float32),
            pltpu.SemaphoreType.DMA((owners,)),
            pltpu.SemaphoreType.DMA((owners,)),
        ],
        compiler_params=pltpu.CompilerParams(collective_id=1, has_side_effects=True),
        name="scatter_sum",
    )(parts)


def ground_kernel(chunk, rays, owners, spectrum_ref, absorption_ref, count_ref, layer_ref,
                  length_ref, weight_ref, ground_ref, out_ref, left, total):
    freqs = absorption_ref.shape[0]
    layers = absorption_ref.shape[1]
    observers = spectrum_ref.shape[1]
    low_size = out_ref.shape[2]
    real, imaginary = spectrum_ref[0:freqs, :], spectrum_ref[freqs : 2 * freqs, :]
    power = real * real + imaginary * imaginary
    highest = lax.Precision.HIGHEST

    def step(index, carry):
        at = pl.ds(pl.multiple_of(index * chunk, chunk), chunk)
        layer_ids = lax.broadcasted_iota(jnp.int32, (layers, chunk), 0)
        count = count_ref[0:1, at]
        lengths = jnp.zeros((layers, chunk), jnp.float32)
        for segment in range(layer_ref.shape[0]):
            used = jnp.where(segment < count, length_ref[segment : segment + 1, at], 0.0)
            same = layer_ref[segment : segment + 1, at] == layer_ids
            lengths = lengths + jnp.where(same, used, 0.0)
        depth = jnp.dot(
            absorption_ref[...], lengths, precision=highest, preferred_element_type=jnp.float32
        )
        shape = (observers, chunk)
        start = lax.broadcasted_iota(jnp.int32, shape, 0) * rays - index * chunk
        column = lax.broadcasted_iota(jnp.int32, shape, 1)
        owner = jnp.where((column >= start) & (column < start + rays), 1.0, 0.0)
        spread = jnp.dot(power, owner, precision=highest, preferred_element_type=jnp.float32)
        energy = spread * weight_ref[0:1, at] * jnp.exp(-depth)
        high = energy.astype(jnp.bfloat16)
        low = (energy - high.astype(jnp.float32)).astype(jnp.bfloat16)
        ground = ground_ref[0:1, at]
        block = ground // low_size
        within = ground - block * low_size
        for owner_id in range(owners):
            keep = jnp.where(block == owner_id, 1.0, 0.0).astype(jnp.bfloat16)
            left[2 * owner_id * freqs : (2 * owner_id + 1) * freqs, :] = high * keep
            left[(2 * owner_id + 1) * freqs : (2 * owner_id + 2) * freqs, :] = low * keep
        ids = lax.broadcasted_iota(jnp.int32, (low_size, chunk), 0)
        right = jnp.where(ids == within, 1.0, 0.0).astype(jnp.bfloat16)
        product = lax.dot_general(
            left[...], right, (((1,), (1,)), ((), ())), preferred_element_type=jnp.float32
        )
        total[...] = product + jnp.where(index > 0, total[...], 0.0)
        return carry

    lax.fori_loop(0, count_ref.shape[1] // chunk, step, 0)
    for owner_id in range(owners):
        first = 2 * owner_id * freqs
        out_ref[owner_id] = total[first : first + freqs, :] + total[
            first + freqs : first + 2 * freqs, :
        ]


def ground_parts(spectrum, absorption, count, layer, length, weight, ground, owners):
    freqs = absorption.shape[0]
    rows = count.shape[1]
    chunk = 1024
    low_size = GROUND // owners
    rays = rows // spectrum.shape[1]
    return pl.pallas_call(
        functools.partial(ground_kernel, chunk, rays, owners),
        out_shape=jax.ShapeDtypeStruct((owners, freqs, low_size), jnp.float32),
        in_specs=[pl.BlockSpec(memory_space=VMEM)] * 7,
        out_specs=pl.BlockSpec(memory_space=VMEM),
        scratch_shapes=[
            pltpu.VMEM((2 * owners * freqs, chunk), jnp.bfloat16),
            pltpu.VMEM((2 * owners * freqs, low_size), jnp.float32),
        ],
        compiler_params=pltpu.CompilerParams(vmem_limit_bytes=48 * 1024 * 1024),
        name="ground",
    )(spectrum, absorption, count, layer, length, weight, ground)


def ground_sum_kernel(owners, groups, part_ref, out_ref, landed, mine, others, send_sem, recv_sem,
                      send_group, recv_group):
    me = lax.axis_index("panel")
    group = lax.axis_index("freq")
    freqs = part_ref.shape[1]
    barrier = enter("panel", owners)
    enter("freq", groups)
    pl.semaphore_wait(barrier, owners + groups - 2)
    copies = []
    for step in range(1, owners):
        peer = lax.rem(me + step, owners)
        copies.append(
            pltpu.make_async_remote_copy(
                src_ref=part_ref.at[peer],
                dst_ref=landed.at[step],
                send_sem=send_sem.at[step],
                recv_sem=recv_sem.at[step],
                device_id={"panel": peer},
                device_id_type=MESH,
            )
        )
        copies[-1].start()
    total = part_ref[me]
    for step in range(1, owners):
        copies[step - 1].wait_recv()
        total = total + landed[step]
    mine[...] = total
    across = []
    for step in range(1, groups):
        peer = lax.rem(group + step, groups)
        across.append(
            pltpu.make_async_remote_copy(
                src_ref=mine,
                dst_ref=others.at[step],
                send_sem=send_group.at[step],
                recv_sem=recv_group.at[step],
                device_id={"freq": peer},
                device_id_type=MESH,
            )
        )
        across[-1].start()
    out_ref[pl.ds(pl.multiple_of(group * freqs, freqs), freqs), :] = total
    for copy in copies:
        copy.wait_send()
    for step in range(1, groups):
        across[step - 1].wait_recv()
        source = lax.rem(group + groups - step, groups)
        out_ref[pl.ds(pl.multiple_of(source * freqs, freqs), freqs), :] = others[step]
    for copy in across:
        copy.wait_send()


def ground_sum(parts, groups):
    owners, freqs, lanes = parts.shape
    return pl.pallas_call(
        functools.partial(ground_sum_kernel, owners, groups),
        out_shape=jax.ShapeDtypeStruct((groups * freqs, lanes), jnp.float32),
        in_specs=[pl.BlockSpec(memory_space=VMEM)],
        out_specs=pl.BlockSpec(memory_space=VMEM),
        scratch_shapes=[
            pltpu.VMEM((owners, freqs, lanes), jnp.float32),
            pltpu.VMEM((freqs, lanes), jnp.float32),
            pltpu.VMEM((groups, freqs, lanes), jnp.float32),
            pltpu.SemaphoreType.DMA((owners,)),
            pltpu.SemaphoreType.DMA((owners,)),
            pltpu.SemaphoreType.DMA((groups,)),
            pltpu.SemaphoreType.DMA((groups,)),
        ],
        compiler_params=pltpu.CompilerParams(collective_id=2, has_side_effects=True),
        name="ground_sum",
    )(parts)


def coefficients(spectra, positions, normals, wavenumbers, weighting):
    mono_real, mono_imag, load_real, load_imag = spectra
    wave = (weighting * wavenumbers)[:, None, None]
    distance = jnp.concatenate(
        [1.0 + jnp.sum(positions * positions, axis=0, keepdims=True), -2.0 * positions]
    )[None]
    facing = jnp.concatenate(
        [-jnp.sum(normals * positions, axis=0, keepdims=True), normals]
    )[None]
    near = weighting / RADIUS
    cube_real = -wave * mono_imag[:, None] * distance + near * load_real[:, None] * facing
    cube_imag = wave * mono_real[:, None] * distance + near * load_imag[:, None] * facing
    square_real = -wave * load_imag[:, None] * facing
    square_imag = wave * load_real[:, None] * facing
    real_rows = jnp.concatenate([cube_real, cube_imag, square_real, square_imag], axis=2)
    imag_rows = jnp.concatenate([cube_imag, -cube_real, square_imag, -square_real], axis=2)
    rows = jnp.concatenate([real_rows, imag_rows], axis=1)
    high = lax.reduce_precision(rows, 8, 7)
    return jnp.concatenate([high, rows - high], axis=1).astype(jnp.bfloat16)


def shards(
    sources,
    panel_pos,
    normal_angles,
    observer_angles,
    absorption,
    ray_count,
    ray_layer,
    ray_length,
    ray_weight,
    ray_ground,
):
    groups = lax.axis_size("freq")
    owners = lax.axis_size("panel")
    freqs = absorption.shape[0] // groups
    freq_start = lax.axis_index("freq") * freqs
    table = jnp.asarray(dft_rows(SAMPLES, BIN0, groups, freqs)).astype(jnp.bfloat16)
    partial_value = lax.dot_general(
        table,
        sources.reshape(-1, SAMPLES),
        (((1,), (1,)), ((), ())),
        preferred_element_type=jnp.float32,
    )
    partial_value = partial_value.reshape(2 * groups * freqs, 2, sources.shape[1])
    spectra = lax.all_to_all(partial_value, "freq", split_axis=0, concat_axis=2, tiled=True)
    spectra = (
        spectra[:freqs, 0],
        spectra[freqs:, 0],
        spectra[:freqs, 1],
        spectra[freqs:, 1],
    )
    first = (BIN0 + freq_start).astype(jnp.float32)
    wavenumbers = (first + jnp.arange(freqs, dtype=jnp.float32)) * (2.0 * math.pi / SAMPLES)
    directions = sphere_points(observer_angles, True)
    normals = sphere_points(normal_angles, False)
    positions = panel_pos / RADIUS
    weighting = GAIN / math.sqrt(panel_pos.shape[1] * owners)
    coefs = coefficients(spectra, positions, normals, wavenumbers, weighting)
    ones = jnp.ones((1, directions.shape[1]), jnp.float32)
    points = jnp.concatenate(
        [directions, jnp.zeros((5, directions.shape[1]), jnp.float32)]
        + [ones, directions, ones, directions]
    )
    padded = jnp.pad(positions.T, ((0, 0), (0, 5)))
    parts = radiate(jnp.full((8, 128), first), padded, points, coefs, owners)
    spectrum = scatter_sum(parts)
    obs_spectrum = (
        spectrum.reshape(2, freqs, -1).transpose(2, 1, 0).reshape(-1, 2 * freqs)
    )
    own_absorption = lax.dynamic_slice_in_dim(absorption, freq_start, freqs, 0)
    ground_part = ground_parts(
        spectrum,
        own_absorption,
        ray_count.reshape(1, -1),
        ray_layer,
        ray_length,
        ray_weight.reshape(1, -1),
        ray_ground.reshape(1, -1),
        owners,
    )
    ground_power = ground_sum(ground_part, groups)
    return (obs_spectrum, ground_power)


def solution(mesh):
    return jax.shard_map(
        shards,
        mesh=mesh,
        in_specs=(
            P(None, ("panel", "freq"), None),
            P(None, "panel"),
            P(None, "panel"),
            P(),
            P(),
            P("panel"),
            P(None, "panel"),
            P(None, "panel"),
            P("panel"),
            P("panel"),
        ),
        out_specs=(P("panel", "freq"), P(None, "panel")),
        check_vma=False,
    )
```

```python
import functools
import math

import jax
import jax.numpy as jnp
import numpy as np
from jax import lax
from jax.experimental import pallas as pl
from jax.experimental.pallas import tpu as pltpu
from jax.sharding import PartitionSpec as P

SAMPLES = 1024
BIN0 = 32
RADIUS = 150.0
GAIN = 3.0
GROUND = 4096
TILE = 16
MESH = pl.DeviceIdType.MESH
VMEM = pltpu.MemorySpace.VMEM


def dft_rows(samples, first_bin, groups, per_group):
    index = np.arange(samples)
    bins = first_bin + np.arange(groups * per_group)
    angle = 2.0 * np.pi / samples * (bins[:, None] * index[None, :] % samples)
    window = (0.5 - 0.5 * np.cos(2.0 * np.pi / samples * index)) / math.sqrt(samples)
    rows = np.stack([window * np.cos(angle), -window * np.sin(angle)])
    rows = rows.reshape(2, groups, per_group, samples).transpose(1, 0, 2, 3)
    return rows.reshape(-1, samples).astype(np.float32)


def sphere_points(angles, downward):
    polar, azimuth = angles[0], angles[1]
    height = -jnp.cos(polar) if downward else jnp.cos(polar)
    return jnp.stack(
        [jnp.sin(polar) * jnp.cos(azimuth), jnp.sin(polar) * jnp.sin(azimuth), height]
    )


def sincos_turns(turns):
    part = turns - jnp.round(turns)
    square = part * part
    sine = jnp.float32(-(math.pi**11) / math.factorial(11))
    for power in (9, 7, 5, 3, 1):
        sign = 1.0 if power % 4 == 1 else -1.0
        sine = sine * square + sign * math.pi**power / math.factorial(power)
    sine = sine * part
    cosine = jnp.float32(math.pi**12 / math.factorial(12))
    for power in (10, 8, 6, 4, 2, 0):
        sign = 1.0 if power % 4 == 0 else -1.0
        cosine = cosine * square + sign * math.pi**power / math.factorial(power)
    return 1.0 - 2.0 * sine * sine, 2.0 * sine * cosine


def enter(axis, count):
    barrier = pltpu.get_barrier_semaphore()
    me = lax.axis_index(axis)
    for step in range(1, count):
        pl.semaphore_signal(
            barrier, inc=1, device_id={axis: lax.rem(me + step, count)}, device_id_type=MESH
        )
    return barrier


def radiate_kernel(freqs, panels, width, blocks, pos_ref, points_ref, coef_ref, out_ref,
                   planes_a, planes_b, stage, parts, landed, send_sem, recv_sem):
    tiles = panels // TILE
    owners, _, lanes = parts.shape
    half = width // lanes
    me = lax.axis_index("panel")
    first = (BIN0 + lax.axis_index("freq") * freqs).astype(jnp.float32)
    start = lax.div(me, half) + 1
    barrier = enter("panel", owners)

    def block_of(order):
        return lax.rem(start + order, blocks)

    def transfer(source, target):
        return pltpu.make_async_remote_copy(
            src_ref=parts.at[target],
            dst_ref=landed.at[source],
            send_sem=send_sem.at[target],
            recv_sem=recv_sem.at[source],
            device_id={"panel": target},
            device_id_type=MESH,
        )

    def generate(planes, order, tile):
        rows = pl.ds(pl.multiple_of(tile * TILE, TILE), TILE)
        cols = pl.ds(pl.multiple_of(block_of(order) * width, width), width)
        total = None
        for axis in range(3):
            diff = points_ref[axis : axis + 1, cols] - pos_ref[rows, axis : axis + 1]
            total = diff * diff if total is None else total + diff * diff
        inverse = lax.rsqrt(total)
        inverse = inverse * (1.5 - 0.5 * total * inverse * inverse)
        turn = total * inverse * jnp.float32(RADIUS / SAMPLES)
        cos_step, sin_step = sincos_turns(turn)
        cos_now, sin_now = sincos_turns(turn * first)
        square = inverse * inverse
        cos_now, sin_now = cos_now * square, sin_now * square
        cos_next = cos_now * cos_step - sin_now * sin_step
        sin_next = sin_now * cos_step + cos_now * sin_step
        twice = 2.0 * cos_step
        for f in range(freqs):
            values = [cos_now * inverse, sin_now * inverse, cos_now, sin_now]
            for part in range(4):
                at = pl.ds(pl.multiple_of(part * panels + tile * TILE, TILE), TILE)
                planes[f, at, :] = values[part].astype(jnp.bfloat16)
            if f + 1 < freqs:
                cos_now, cos_next = cos_next, twice * cos_next - cos_now
                sin_now, sin_next = sin_next, twice * sin_next - sin_now

    def contract(planes, order, f):
        cols = pl.ds(pl.multiple_of(block_of(order) * width, width), width)
        product = jnp.dot(coef_ref[f], planes[f], preferred_element_type=jnp.float32)
        product = (product[0:8] + product[8:16]) * points_ref[8:16, cols]
        product = product + pltpu.roll(product, 1, axis=0)
        product = product + pltpu.roll(product, 2, axis=0)
        for side in range(half):
            stage[side, pl.ds(pl.multiple_of(f * 8, 8), 8), :] = product[
                :, side * lanes : (side + 1) * lanes
            ]

    def finish(order):
        for side in range(half):
            target = block_of(order) * half + side
            for part in range(2):
                parts[target, part * freqs : (part + 1) * freqs, :] = stage[
                    side, pl.ds(4 * part + 3, freqs, 8), :
                ]

            @pl.when(target != me)
            def _():
                transfer(me, target).start()

    def phase(generated, generated_order, used, used_order):
        if generated is not None and used is not None and freqs % tiles == 0:
            each = freqs // tiles

            def both(tile, carry):
                for n in range(each):
                    contract(used, used_order, tile * each + n)
                generate(generated, generated_order, tile)
                return carry

            lax.fori_loop(0, tiles, both, 0)
            finish(used_order)
            return
        if generated is not None:

            def only_generate(tile, carry):
                generate(generated, generated_order, tile)
                return carry

            lax.fori_loop(0, tiles, only_generate, 0)
        if used is not None:

            def only_contract(f, carry):
                contract(used, used_order, f)
                return carry

            lax.fori_loop(0, freqs, only_contract, 0)
            finish(used_order)

    phase(planes_a, 0, None, None)
    pl.semaphore_wait(barrier, owners - 1)

    def pair(step, carry):
        phase(planes_b, 2 * step + 1, planes_a, 2 * step)
        phase(planes_a, 2 * step + 2, planes_b, 2 * step + 1)
        return carry

    lax.fori_loop(0, blocks // 2 - 1, pair, 0)
    phase(planes_b, blocks - 1, planes_a, blocks - 2)
    phase(None, None, planes_b, blocks - 1)
    total = parts[me]
    for step in range(1, owners):
        source = lax.rem(me + step, owners)
        transfer(source, source).wait_recv()
        total = total + landed[source]
    out_ref[...] = total
    for step in range(1, owners):
        target = lax.rem(me + step, owners)
        transfer(target, target).wait_send()


def radiate(positions, points, coefs, owners):
    freqs, _, depth = coefs.shape
    panels = depth // 4
    observers = points.shape[1]
    lanes = observers // owners
    width = 256
    blocks = observers // width
    return pl.pallas_call(
        functools.partial(radiate_kernel, freqs, panels, width, blocks),
        out_shape=jax.ShapeDtypeStruct((2 * freqs, lanes), jnp.float32),
        in_specs=[pl.BlockSpec(memory_space=VMEM)] * 3,
        out_specs=pl.BlockSpec(memory_space=VMEM),
        scratch_shapes=[
            pltpu.VMEM((freqs, depth, width), jnp.bfloat16),
            pltpu.VMEM((freqs, depth, width), jnp.bfloat16),
            pltpu.VMEM((width // lanes, freqs * 8, lanes), jnp.float32),
            pltpu.VMEM((owners, 2 * freqs, lanes), jnp.float32),
            pltpu.VMEM((owners, 2 * freqs, lanes), jnp.float32),
            pltpu.SemaphoreType.DMA((owners,)),
            pltpu.SemaphoreType.DMA((owners,)),
        ],
        compiler_params=pltpu.CompilerParams(
            vmem_limit_bytes=60 * 1024 * 1024, collective_id=1, has_side_effects=True
        ),
        name="radiate",
    )(positions, points, coefs)


def ground_kernel(chunk, rays, owners, groups, each, spectrum_ref, absorption_ref, count_ref,
                  layer_ref, length_ref, weight_ref, ground_ref, out_ref, energies, lows, left,
                  total, own, parts, landed, mine, others, send_sem, recv_sem, send_group,
                  recv_group):
    freqs = absorption_ref.shape[0]
    layers = absorption_ref.shape[1]
    observers = spectrum_ref.shape[1]
    low_size = out_ref.shape[1]
    me = lax.axis_index("panel")
    group = lax.axis_index("freq")
    barrier = enter("panel", owners)
    enter("freq", groups)
    real, imaginary = spectrum_ref[0:freqs, :], spectrum_ref[freqs : 2 * freqs, :]
    power = real * real + imaginary * imaginary
    highest = lax.Precision.HIGHEST
    chunks = count_ref.shape[1] // chunk

    def transfer(source, target):
        return pltpu.make_async_remote_copy(
            src_ref=parts.at[target],
            dst_ref=landed.at[source],
            send_sem=send_sem.at[target],
            recv_sem=recv_sem.at[source],
            device_id={"panel": target},
            device_id_type=MESH,
        )

    def prepare(index, carry):
        at = pl.ds(pl.multiple_of(index * chunk, chunk), chunk)
        layer_ids = lax.broadcasted_iota(jnp.int32, (layers, chunk), 0)
        count = count_ref[0:1, at]
        lengths = jnp.zeros((layers, chunk), jnp.float32)
        for segment in range(layer_ref.shape[0]):
            used = jnp.where(segment < count, length_ref[segment : segment + 1, at], 0.0)
            same = layer_ref[segment : segment + 1, at] == layer_ids
            lengths = lengths + jnp.where(same, used, 0.0)
        depth = jnp.dot(
            absorption_ref[...], lengths, precision=highest, preferred_element_type=jnp.float32
        )
        shape = (observers, chunk)
        start = lax.broadcasted_iota(jnp.int32, shape, 0) * rays - index * chunk
        column = lax.broadcasted_iota(jnp.int32, shape, 1)
        owner = jnp.where((column >= start) & (column < start + rays), 1.0, 0.0)
        spread = jnp.dot(power, owner, precision=highest, preferred_element_type=jnp.float32)
        energy = spread * weight_ref[0:1, at] * jnp.exp(-depth)
        high = energy.astype(jnp.bfloat16)
        energies[0:freqs, at] = high
        energies[freqs : 2 * freqs, at] = (energy - high.astype(jnp.float32)).astype(jnp.bfloat16)
        within = ground_ref[0:1, at] & (low_size - 1)
        ids = lax.broadcasted_iota(jnp.int32, (low_size, chunk), 0)
        lows[:, at] = jnp.where(ids == within, 1.0, 0.0).astype(jnp.bfloat16)
        return carry

    lax.fori_loop(0, chunks, prepare, 0)
    pl.semaphore_wait(barrier, owners + groups - 2)

    def batch(order, carry):
        base = lax.rem(lax.div(me, each) + 1 + order, owners // each) * each
        total[...] = jnp.zeros_like(total)

        def step(index, carry):
            at = pl.ds(pl.multiple_of(index * chunk, chunk), chunk)
            block = ground_ref[0:1, at] // low_size
            for n in range(each):
                keep = jnp.where(block == base + n, 1.0, 0.0).astype(jnp.bfloat16)
                left[2 * n * freqs : 2 * (n + 1) * freqs, :] = energies[:, at] * keep
            total[...] += lax.dot_general(
                left[...],
                lows[:, at],
                (((1,), (1,)), ((), ())),
                preferred_element_type=jnp.float32,
            )
            return carry

        lax.fori_loop(0, chunks, step, 0)
        for n in range(each):
            target = base + n
            middle = (2 * n + 1) * freqs
            value = total[middle - freqs : middle, :] + total[middle : middle + freqs, :]
            parts[target] = value.astype(jnp.bfloat16)

            @pl.when(target != me)
            def _():
                transfer(me, target).start()

            @pl.when(target == me)
            def _():
                own[...] = value

        return carry

    lax.fori_loop(0, owners // each, batch, 0)
    value = own[...]
    for step in range(1, owners):
        source = lax.rem(me + step, owners)
        transfer(source, source).wait_recv()
        value = value + landed[source].astype(jnp.float32)
    mine[...] = value
    across = []
    for step in range(1, groups):
        peer = lax.rem(group + step, groups)
        across.append(
            pltpu.make_async_remote_copy(
                src_ref=mine,
                dst_ref=others.at[step],
                send_sem=send_group.at[step],
                recv_sem=recv_group.at[step],
                device_id={"freq": peer},
                device_id_type=MESH,
            )
        )
        across[-1].start()
    out_ref[pl.ds(pl.multiple_of(group * freqs, freqs), freqs), :] = value
    for step in range(1, owners):
        target = lax.rem(me + step, owners)
        transfer(target, target).wait_send()
    for step in range(1, groups):
        across[step - 1].wait_recv()
        source = lax.rem(group + groups - step, groups)
        out_ref[pl.ds(pl.multiple_of(source * freqs, freqs), freqs), :] = others[step]
    for copy in across:
        copy.wait_send()


def ground_sums(spectrum, absorption, count, layer, length, weight, ground, owners, groups):
    freqs = absorption.shape[0]
    rows = count.shape[1]
    chunk = 1024
    low_size = GROUND // owners
    rays = rows // spectrum.shape[1]
    each = min(4, owners)
    return pl.pallas_call(
        functools.partial(ground_kernel, chunk, rays, owners, groups, each),
        out_shape=jax.ShapeDtypeStruct((groups * freqs, low_size), jnp.float32),
        in_specs=[pl.BlockSpec(memory_space=VMEM)] * 7,
        out_specs=pl.BlockSpec(memory_space=VMEM),
        scratch_shapes=[
            pltpu.VMEM((2 * freqs, rows), jnp.bfloat16),
            pltpu.VMEM((low_size, rows), jnp.bfloat16),
            pltpu.VMEM((2 * each * freqs, chunk), jnp.bfloat16),
            pltpu.VMEM((2 * each * freqs, low_size), jnp.float32),
            pltpu.VMEM((freqs, low_size), jnp.float32),
            pltpu.VMEM((owners, freqs, low_size), jnp.bfloat16),
            pltpu.VMEM((owners, freqs, low_size), jnp.bfloat16),
            pltpu.VMEM((freqs, low_size), jnp.float32),
            pltpu.VMEM((groups, freqs, low_size), jnp.float32),
            pltpu.SemaphoreType.DMA((owners,)),
            pltpu.SemaphoreType.DMA((owners,)),
            pltpu.SemaphoreType.DMA((groups,)),
            pltpu.SemaphoreType.DMA((groups,)),
        ],
        compiler_params=pltpu.CompilerParams(
            vmem_limit_bytes=48 * 1024 * 1024, collective_id=2, has_side_effects=True
        ),
        name="ground",
    )(spectrum, absorption, count, layer, length, weight, ground)


def coefficients(spectra, positions, normals, wavenumbers, weighting):
    mono_real, mono_imag, load_real, load_imag = spectra
    wave = (weighting * wavenumbers)[:, None, None]
    distance = jnp.concatenate(
        [1.0 + jnp.sum(positions * positions, axis=0, keepdims=True), -2.0 * positions]
    )[None]
    facing = jnp.concatenate(
        [-jnp.sum(normals * positions, axis=0, keepdims=True), normals]
    )[None]
    near = weighting / RADIUS
    cube_real = -wave * mono_imag[:, None] * distance + near * load_real[:, None] * facing
    cube_imag = wave * mono_real[:, None] * distance + near * load_imag[:, None] * facing
    square_real = -wave * load_imag[:, None] * facing
    square_imag = wave * load_real[:, None] * facing
    real_rows = jnp.concatenate([cube_real, cube_imag, square_real, square_imag], axis=2)
    imag_rows = jnp.concatenate([cube_imag, -cube_real, square_imag, -square_real], axis=2)
    rows = jnp.concatenate([real_rows, imag_rows], axis=1)
    high = lax.reduce_precision(rows, 8, 7)
    return jnp.concatenate([high, rows - high], axis=1).astype(jnp.bfloat16)


def shards(
    sources,
    panel_pos,
    normal_angles,
    observer_angles,
    absorption,
    ray_count,
    ray_layer,
    ray_length,
    ray_weight,
    ray_ground,
):
    groups = lax.axis_size("freq")
    owners = lax.axis_size("panel")
    freqs = absorption.shape[0] // groups
    freq_start = lax.axis_index("freq") * freqs
    table = jnp.asarray(dft_rows(SAMPLES, BIN0, groups, freqs)).astype(jnp.bfloat16)
    partial_value = lax.dot_general(
        table,
        sources.reshape(-1, SAMPLES),
        (((1,), (1,)), ((), ())),
        preferred_element_type=jnp.float32,
    )
    partial_value = partial_value.reshape(2 * groups * freqs, 2, sources.shape[1])
    spectra = lax.all_to_all(partial_value, "freq", split_axis=0, concat_axis=2, tiled=True)
    spectra = (
        spectra[:freqs, 0],
        spectra[freqs:, 0],
        spectra[:freqs, 1],
        spectra[freqs:, 1],
    )
    first = (BIN0 + freq_start).astype(jnp.float32)
    wavenumbers = (first + jnp.arange(freqs, dtype=jnp.float32)) * (2.0 * math.pi / SAMPLES)
    directions = sphere_points(observer_angles, True)
    normals = sphere_points(normal_angles, False)
    positions = panel_pos / RADIUS
    weighting = GAIN / math.sqrt(panel_pos.shape[1] * owners)
    coefs = coefficients(spectra, positions, normals, wavenumbers, weighting)
    ones = jnp.ones((1, directions.shape[1]), jnp.float32)
    points = jnp.concatenate(
        [directions, jnp.zeros((5, directions.shape[1]), jnp.float32)]
        + [ones, directions, ones, directions]
    )
    spectrum = radiate(positions.T, points, coefs, owners)
    obs_spectrum = (
        spectrum.reshape(2, freqs, -1).transpose(2, 1, 0).reshape(-1, 2 * freqs)
    )
    own_absorption = lax.dynamic_slice_in_dim(absorption, freq_start, freqs, 0)
    ground_power = ground_sums(
        spectrum,
        own_absorption,
        ray_count.reshape(1, -1),
        ray_layer,
        ray_length,
        ray_weight.reshape(1, -1),
        ray_ground.reshape(1, -1),
        owners,
        groups,
    )
    return (obs_spectrum, ground_power)


def solution(mesh):
    return jax.shard_map(
        shards,
        mesh=mesh,
        in_specs=(
            P(None, ("panel", "freq"), None),
            P(None, "panel"),
            P(None, "panel"),
            P(),
            P(),
            P("panel"),
            P(None, "panel"),
            P(None, "panel"),
            P("panel"),
            P("panel"),
        ),
        out_specs=(P("panel", "freq"), P(None, "panel")),
        check_vma=False,
    )
```

```python
import functools
import math

import jax
import jax.numpy as jnp
import numpy as np
from jax import lax
from jax.experimental import pallas as pl
from jax.experimental.pallas import tpu as pltpu
from jax.sharding import PartitionSpec as P

SAMPLES = 1024
BIN0 = 32
RADIUS = 150.0
GAIN = 3.0
GROUND = 4096
TILE = 16
MESH = pl.DeviceIdType.MESH
VMEM = pltpu.MemorySpace.VMEM


def dft_rows(samples, first_bin, groups, per_group):
    index = np.arange(samples)
    bins = first_bin + np.arange(groups * per_group)
    angle = 2.0 * np.pi / samples * (bins[:, None] * index[None, :] % samples)
    window = (0.5 - 0.5 * np.cos(2.0 * np.pi / samples * index)) / math.sqrt(samples)
    rows = np.stack([window * np.cos(angle), -window * np.sin(angle)])
    rows = rows.reshape(2, groups, per_group, samples).transpose(1, 0, 2, 3)
    return rows.reshape(-1, samples).astype(np.float32)


def sphere_points(angles, downward):
    polar, azimuth = angles[0], angles[1]
    height = -jnp.cos(polar) if downward else jnp.cos(polar)
    return jnp.stack(
        [jnp.sin(polar) * jnp.cos(azimuth), jnp.sin(polar) * jnp.sin(azimuth), height]
    )


def sincos_turns(turns):
    part = turns - jnp.round(turns)
    square = part * part
    sine = jnp.float32(-(math.pi**11) / math.factorial(11))
    for power in (9, 7, 5, 3, 1):
        sign = 1.0 if power % 4 == 1 else -1.0
        sine = sine * square + sign * math.pi**power / math.factorial(power)
    sine = sine * part
    cosine = jnp.float32(math.pi**12 / math.factorial(12))
    for power in (10, 8, 6, 4, 2, 0):
        sign = 1.0 if power % 4 == 0 else -1.0
        cosine = cosine * square + sign * math.pi**power / math.factorial(power)
    return 1.0 - 2.0 * sine * sine, 2.0 * sine * cosine


def enter(axis, count):
    barrier = pltpu.get_barrier_semaphore()
    me = lax.axis_index(axis)
    for step in range(1, count):
        pl.semaphore_signal(
            barrier, inc=1, device_id={axis: lax.rem(me + step, count)}, device_id_type=MESH
        )
    return barrier


def split_float(value):
    pieces = []
    for _ in range(3):
        pieces.append(value.astype(jnp.bfloat16))
        value = value - pieces[-1].astype(jnp.float32)
    return pieces


def radiate_kernel(freqs, panels, width, blocks, pos_ref, directions_ref, coef_ref, out_ref,
                   points_ref, planes_a, planes_b, stage, parts, landed, send_sem, recv_sem):
    tiles = panels // TILE
    owners, _, lanes = parts.shape
    half = width // lanes
    me = lax.axis_index("panel")
    first = (BIN0 + lax.axis_index("freq") * freqs).astype(jnp.float32)
    start = lax.div(me, half) + 1
    barrier = enter("panel", owners)

    def block_of(order):
        return lax.rem(start + order, blocks)

    def transfer(source, target):
        return pltpu.make_async_remote_copy(
            src_ref=parts.at[target],
            dst_ref=landed.at[source],
            send_sem=send_sem.at[target],
            recv_sem=recv_sem.at[source],
            device_id={"panel": target},
            device_id_type=MESH,
        )

    def generate(planes, order, tile):
        rows = pl.ds(pl.multiple_of(tile * TILE, TILE), TILE)
        cols = pl.ds(pl.multiple_of(block_of(order) * width, width), width)
        total = None
        for axis in range(3):
            diff = points_ref[axis : axis + 1, cols] - pos_ref[rows, axis : axis + 1]
            total = diff * diff if total is None else total + diff * diff
        inverse = lax.rsqrt(total)
        inverse = inverse * (1.5 - 0.5 * total * inverse * inverse)
        turn = total * inverse * jnp.float32(RADIUS / SAMPLES)
        cos_step, sin_step = sincos_turns(turn)
        cos_now, sin_now = sincos_turns(turn * first)
        square = inverse * inverse
        cos_now, sin_now = cos_now * square, sin_now * square
        cos_next = cos_now * cos_step - sin_now * sin_step
        sin_next = sin_now * cos_step + cos_now * sin_step
        twice = 2.0 * cos_step
        for f in range(freqs):
            values = [cos_now * inverse, sin_now * inverse, cos_now, sin_now]
            for part in range(4):
                at = pl.ds(pl.multiple_of(part * panels + tile * TILE, TILE), TILE)
                planes[f, at, :] = values[part].astype(jnp.bfloat16)
            if f + 1 < freqs:
                cos_now, cos_next = cos_next, twice * cos_next - cos_now
                sin_now, sin_next = sin_next, twice * sin_next - sin_now

    def contract(planes, order, f):
        cols = pl.ds(pl.multiple_of(block_of(order) * width, width), width)
        product = jnp.dot(coef_ref[f], planes[f], preferred_element_type=jnp.float32)
        product = (product[0:8] + product[8:16]) * points_ref[8:16, cols]
        product = product + pltpu.roll(product, 1, axis=0)
        product = product + pltpu.roll(product, 2, axis=0)
        for side in range(half):
            stage[side, pl.ds(pl.multiple_of(f * 8, 8), 8), :] = product[
                :, side * lanes : (side + 1) * lanes
            ]

    def finish(order):
        for side in range(half):
            target = block_of(order) * half + side
            for part in range(2):
                parts[target, part * freqs : (part + 1) * freqs, :] = stage[
                    side, pl.ds(4 * part + 3, freqs, 8), :
                ]

            @pl.when(target != me)
            def _():
                transfer(me, target).start()

    def phase(generated, generated_order, used, used_order):
        if generated is not None and used is not None and freqs % tiles == 0:
            each = freqs // tiles

            def both(tile, carry):
                for n in range(each):
                    contract(used, used_order, tile * each + n)
                generate(generated, generated_order, tile)
                return carry

            lax.fori_loop(0, tiles, both, 0)
            finish(used_order)
            return
        if generated is not None:

            def only_generate(tile, carry):
                generate(generated, generated_order, tile)
                return carry

            lax.fori_loop(0, tiles, only_generate, 0)
        if used is not None:

            def only_contract(f, carry):
                contract(used, used_order, f)
                return carry

            lax.fori_loop(0, freqs, only_contract, 0)
            finish(used_order)

    directions = directions_ref[...]
    points_ref[0:3, :] = directions
    for row in (8, 12):
        points_ref[row : row + 1, :] = jnp.ones_like(directions[0:1])
        points_ref[row + 1 : row + 4, :] = directions
    phase(planes_a, 0, None, None)
    pl.semaphore_wait(barrier, owners - 1)

    def pair(step, carry):
        phase(planes_b, 2 * step + 1, planes_a, 2 * step)
        phase(planes_a, 2 * step + 2, planes_b, 2 * step + 1)
        return carry

    lax.fori_loop(0, blocks // 2 - 1, pair, 0)
    phase(planes_b, blocks - 1, planes_a, blocks - 2)
    phase(None, None, planes_b, blocks - 1)
    total = parts[me]
    for step in range(1, owners):
        source = lax.rem(me + step, owners)
        transfer(source, source).wait_recv()
        total = total + landed[source]
    out_ref[...] = total
    for step in range(1, owners):
        target = lax.rem(me + step, owners)
        transfer(target, target).wait_send()


def radiate(positions, directions, coefs, owners):
    freqs, _, depth = coefs.shape
    panels = depth // 4
    observers = directions.shape[1]
    lanes = observers // owners
    width = 256
    blocks = observers // width
    return pl.pallas_call(
        functools.partial(radiate_kernel, freqs, panels, width, blocks),
        out_shape=jax.ShapeDtypeStruct((2 * freqs, lanes), jnp.float32),
        in_specs=[pl.BlockSpec(memory_space=VMEM)] * 3,
        out_specs=pl.BlockSpec(memory_space=VMEM),
        scratch_shapes=[
            pltpu.VMEM((16, observers), jnp.float32),
            pltpu.VMEM((freqs, depth, width), jnp.bfloat16),
            pltpu.VMEM((freqs, depth, width), jnp.bfloat16),
            pltpu.VMEM((width // lanes, freqs * 8, lanes), jnp.float32),
            pltpu.VMEM((owners, 2 * freqs, lanes), jnp.float32),
            pltpu.VMEM((owners, 2 * freqs, lanes), jnp.float32),
            pltpu.SemaphoreType.DMA((owners,)),
            pltpu.SemaphoreType.DMA((owners,)),
        ],
        compiler_params=pltpu.CompilerParams(
            vmem_limit_bytes=60 * 1024 * 1024,
            collective_id=1,
            has_side_effects=True,
        ),
        name="radiate",
    )(positions, directions, coefs)


def ground_kernel(chunk, rays, owners, groups, each, spectrum_ref, absorption_ref, count_ref,
                  layer_ref, length_ref, weight_ref, ground_ref, out_ref, spreading, energies, lows, left,
                  total, own, parts, landed, mine, others, send_sem, recv_sem, send_group,
                  recv_group):
    freqs = absorption_ref.shape[0]
    layers = absorption_ref.shape[1]
    observers = spectrum_ref.shape[1]
    low_size = out_ref.shape[1]
    me = lax.axis_index("panel")
    group = lax.axis_index("freq")
    barrier = enter("panel", owners)
    enter("freq", groups)
    real, imaginary = spectrum_ref[0:freqs, :], spectrum_ref[freqs : 2 * freqs, :]
    power = real * real + imaginary * imaginary
    chunks = count_ref.shape[1] // chunk
    split = split_float(absorption_ref[...])
    absorb = jnp.concatenate([split[i] for i in (0, 0, 1, 0, 1, 2)], axis=1)
    shape = (observers, chunk)
    begin = lax.broadcasted_iota(jnp.int32, shape, 0) * rays
    column = lax.broadcasted_iota(jnp.int32, shape, 1)
    same_owner = (column >= begin) & (column < begin + rays)
    spreading[...] = jnp.where(same_owner, 1.0, 0.0).astype(jnp.bfloat16)

    def transfer(source, target):
        return pltpu.make_async_remote_copy(
            src_ref=parts.at[target],
            dst_ref=landed.at[source],
            send_sem=send_sem.at[target],
            recv_sem=recv_sem.at[source],
            device_id={"panel": target},
            device_id_type=MESH,
        )

    def prepare(index, carry):
        at = pl.ds(pl.multiple_of(index * chunk, chunk), chunk)
        layer_ids = lax.broadcasted_iota(jnp.int32, (layers, chunk), 0)
        count = count_ref[0:1, at]
        lengths = jnp.zeros((layers, chunk), jnp.float32)
        for segment in range(layer_ref.shape[0]):
            used = jnp.where(segment < count, length_ref[segment : segment + 1, at], 0.0)
            same = layer_ref[segment : segment + 1, at] == layer_ids
            lengths = lengths + jnp.where(same, used, 0.0)
        split = split_float(lengths)
        lengths = jnp.concatenate([split[i] for i in (0, 1, 0, 2, 1, 0)], axis=0)
        depth = jnp.dot(absorb, lengths, preferred_element_type=jnp.float32)
        turned = pltpu.roll(power, lax.rem(observers - index * (chunk // rays), observers), axis=1)
        spread = jnp.dot(
            jnp.concatenate(split_float(turned), axis=0),
            spreading[...],
            preferred_element_type=jnp.float32,
        )
        spread = spread[0:freqs] + spread[freqs : 2 * freqs] + spread[2 * freqs : 3 * freqs]
        energy = spread * weight_ref[0:1, at] * jnp.exp(-depth)
        energies[:, at] = energy.astype(jnp.bfloat16)
        within = ground_ref[0:1, at] & (low_size - 1)
        ids = lax.broadcasted_iota(jnp.int32, (low_size, chunk), 0)
        lows[:, at] = jnp.where(ids == within, 1.0, 0.0).astype(jnp.bfloat16)
        return carry

    lax.fori_loop(0, chunks, prepare, 0)
    pl.semaphore_wait(barrier, owners + groups - 2)

    def batch(order, carry):
        base = lax.rem(lax.div(me, each) + 1 + order, owners // each) * each
        total[...] = jnp.zeros_like(total)

        def step(index, carry):
            at = pl.ds(pl.multiple_of(index * chunk, chunk), chunk)
            block = ground_ref[0:1, at] // low_size
            for n in range(each):
                keep = jnp.where(block == base + n, 1.0, 0.0).astype(jnp.bfloat16)
                left[n * freqs : (n + 1) * freqs, :] = energies[:, at] * keep
            total[...] += lax.dot_general(
                left[...],
                lows[:, at],
                (((1,), (1,)), ((), ())),
                preferred_element_type=jnp.float32,
            )
            return carry

        lax.fori_loop(0, chunks, step, 0)
        for n in range(each):
            target = base + n
            value = total[n * freqs : (n + 1) * freqs, :]
            parts[target] = value.astype(jnp.bfloat16)

            @pl.when(target != me)
            def _():
                transfer(me, target).start()

            @pl.when(target == me)
            def _():
                own[...] = value

        return carry

    lax.fori_loop(0, owners // each, batch, 0)
    value = own[...]
    for step in range(1, owners):
        source = lax.rem(me + step, owners)
        transfer(source, source).wait_recv()
        value = value + landed[source].astype(jnp.float32)
    mine[...] = value
    across = []
    for step in range(1, groups):
        peer = lax.rem(group + step, groups)
        across.append(
            pltpu.make_async_remote_copy(
                src_ref=mine,
                dst_ref=others.at[step],
                send_sem=send_group.at[step],
                recv_sem=recv_group.at[step],
                device_id={"freq": peer},
                device_id_type=MESH,
            )
        )
        across[-1].start()
    out_ref[pl.ds(pl.multiple_of(group * freqs, freqs), freqs), :] = value
    for step in range(1, owners):
        target = lax.rem(me + step, owners)
        transfer(target, target).wait_send()
    for step in range(1, groups):
        across[step - 1].wait_recv()
        source = lax.rem(group + groups - step, groups)
        out_ref[pl.ds(pl.multiple_of(source * freqs, freqs), freqs), :] = others[step]
    for copy in across:
        copy.wait_send()


def ground_sums(spectrum, absorption, count, layer, length, weight, ground, owners, groups):
    freqs = absorption.shape[0]
    rows = count.shape[1]
    chunk = 1024
    low_size = GROUND // owners
    rays = rows // spectrum.shape[1]
    each = min(4, owners)
    return pl.pallas_call(
        functools.partial(ground_kernel, chunk, rays, owners, groups, each),
        out_shape=jax.ShapeDtypeStruct((groups * freqs, low_size), jnp.float32),
        in_specs=[pl.BlockSpec(memory_space=VMEM)] * 7,
        out_specs=pl.BlockSpec(memory_space=VMEM),
        scratch_shapes=[
            pltpu.VMEM((spectrum.shape[1], chunk), jnp.bfloat16),
            pltpu.VMEM((freqs, rows), jnp.bfloat16),
            pltpu.VMEM((low_size, rows), jnp.bfloat16),
            pltpu.VMEM((each * freqs, chunk), jnp.bfloat16),
            pltpu.VMEM((each * freqs, low_size), jnp.float32),
            pltpu.VMEM((freqs, low_size), jnp.float32),
            pltpu.VMEM((owners, freqs, low_size), jnp.bfloat16),
            pltpu.VMEM((owners, freqs, low_size), jnp.bfloat16),
            pltpu.VMEM((freqs, low_size), jnp.float32),
            pltpu.VMEM((groups, freqs, low_size), jnp.float32),
            pltpu.SemaphoreType.DMA((owners,)),
            pltpu.SemaphoreType.DMA((owners,)),
            pltpu.SemaphoreType.DMA((groups,)),
            pltpu.SemaphoreType.DMA((groups,)),
        ],
        compiler_params=pltpu.CompilerParams(
            vmem_limit_bytes=48 * 1024 * 1024,
            collective_id=2,
            has_side_effects=True,
        ),
        name="ground",
    )(spectrum, absorption, count, layer, length, weight, ground)


def coefficients(spectra, positions, normals, wavenumbers, weighting):
    mono_real, mono_imag, load_real, load_imag = spectra
    wave = (weighting * wavenumbers)[:, None, None]
    distance = jnp.concatenate(
        [1.0 + jnp.sum(positions * positions, axis=0, keepdims=True), -2.0 * positions]
    )[None]
    facing = jnp.concatenate(
        [-jnp.sum(normals * positions, axis=0, keepdims=True), normals]
    )[None]
    near = weighting / RADIUS
    cube_real = -wave * mono_imag[:, None] * distance + near * load_real[:, None] * facing
    cube_imag = wave * mono_real[:, None] * distance + near * load_imag[:, None] * facing
    square_real = -wave * load_imag[:, None] * facing
    square_imag = wave * load_real[:, None] * facing
    real_rows = jnp.concatenate([cube_real, cube_imag, square_real, square_imag], axis=2)
    imag_rows = jnp.concatenate([cube_imag, -cube_real, square_imag, -square_real], axis=2)
    rows = jnp.concatenate([real_rows, imag_rows], axis=1)
    high = lax.reduce_precision(rows, 8, 7)
    return jnp.concatenate([high, rows - high], axis=1).astype(jnp.bfloat16)


def shards(
    sources,
    panel_pos,
    normal_angles,
    observer_angles,
    absorption,
    ray_count,
    ray_layer,
    ray_length,
    ray_weight,
    ray_ground,
):
    groups = lax.axis_size("freq")
    owners = lax.axis_size("panel")
    freqs = absorption.shape[0] // groups
    freq_start = lax.axis_index("freq") * freqs
    table = jnp.asarray(dft_rows(SAMPLES, BIN0, groups, freqs)).astype(jnp.bfloat16)
    partial_value = lax.dot_general(
        table,
        sources.reshape(-1, SAMPLES),
        (((1,), (1,)), ((), ())),
        preferred_element_type=jnp.float32,
    )
    partial_value = partial_value.reshape(2 * groups * freqs, 2, sources.shape[1])
    spectra = lax.all_to_all(partial_value, "freq", split_axis=0, concat_axis=2, tiled=True)
    spectra = (
        spectra[:freqs, 0],
        spectra[freqs:, 0],
        spectra[:freqs, 1],
        spectra[freqs:, 1],
    )
    first = (BIN0 + freq_start).astype(jnp.float32)
    wavenumbers = (first + jnp.arange(freqs, dtype=jnp.float32)) * (2.0 * math.pi / SAMPLES)
    directions = sphere_points(observer_angles, True)
    normals = sphere_points(normal_angles, False)
    positions = panel_pos / RADIUS
    weighting = GAIN / math.sqrt(panel_pos.shape[1] * owners)
    coefs = coefficients(spectra, positions, normals, wavenumbers, weighting)
    spectrum = radiate(positions.T, directions, coefs, owners)
    obs_spectrum = (
        spectrum.reshape(2, freqs, -1).transpose(2, 1, 0).reshape(-1, 2 * freqs)
    )
    own_absorption = lax.dynamic_slice_in_dim(absorption, freq_start, freqs, 0)
    ground_power = ground_sums(
        spectrum,
        own_absorption,
        ray_count.reshape(1, -1),
        ray_layer,
        ray_length,
        ray_weight.reshape(1, -1),
        ray_ground.reshape(1, -1),
        owners,
        groups,
    )
    return (obs_spectrum, ground_power)


def solution(mesh):
    return jax.shard_map(
        shards,
        mesh=mesh,
        in_specs=(
            P(None, ("panel", "freq"), None),
            P(None, "panel"),
            P(None, "panel"),
            P(),
            P(),
            P("panel"),
            P(None, "panel"),
            P(None, "panel"),
            P("panel"),
            P("panel"),
        ),
        out_specs=(P("panel", "freq"), P(None, "panel")),
        check_vma=False,
    )
```
